128 devices in a mesh: row: 16 (over x, y), col: 8 (over z, core).
Axes of the slice: x: 4, y: 4, z: 4, core: 2. Of those that a mesh axis runs over, the one named last changes fastest.
Arguments:
- raw_rows: bfloat16 [131072, 64], P(('row', 'col')), may hold values from -6 to 6
- raw_wide: int32 [131072], P(('row', 'col')), may hold values from 0 to 1
- raw_dest: int32 [131072], P(('row', 'col')), may hold values from 0 to 127, as said below
- raw_slot: int32 [131072], P(('row', 'col')), may hold values from 0 to 511
- proj_narrow: bfloat16 [32, 128], replicated, may hold values from -1 to 1
- proj_wide: bfloat16 [64, 128], replicated, may hold values from -0.75 to 0.75
- adj_values: bfloat16 [32768, 32768], P('row', 'col'), may hold values from -1 to 1
- tile_mask: int32 [256, 256], P('row', 'col'), may hold values 0 or 1
- tile_scale: float32 [256, 256], P('row', 'col'), may hold values from 0.0041432036 to 0.041432038
- weight_sum: bfloat16 [2, 128, 128], replicated, may hold values from -0.5 to 0.5
- weight_product: bfloat16 [2, 128, 128], replicated, may hold values from -0.5 to 0.5
Outputs:
- user_out: bfloat16 [32768, 128], P(('row', 'col'))
- item_out: bfloat16 [8, 4096, 128], P('col', 'row')
The draws below stay inside these ranges and needn't reach their ends.
Inputs may be any that keep to these rules, and one draw needn't show every extreme that they name: `raw_dest`: among the feature rows stored on one device at most 24 have any one destination; one device, drawn from the seed, is the destination of exactly 24 rows of every device.
All inputs are finite; a program needn't handle non-finite values. No bound on the sum of `tile_mask` on one device may be relied on, other than what follows from the above.
Results may differ from the reference program's by a relative error of at most 0.025.
Values may be sent and summed in bfloat16 or wider, within the bound.
A program may use at most 128 MiB of HBM per device.

```python
import math
import jax
import jax.numpy as jnp
from jax import lax

D = 128
RAW_COLS = 64
NARROW = 32
TILE = 128
LAYERS = 2
UPD = 256
IPD = 256
RAW_DEV = 1024
CAP = 24
NU = 32768
NI = 32768
N_ROW = 16
N_COL = 8
DEVICES = 128


def draw_raw_dest(key, part):
    busiest = jax.random.randint(jax.random.fold_in(key, 11), (), 0, DEVICES)
    source_keys = jax.random.split(jax.random.fold_in(key, 12), DEVICES)

    def one_source(source_key):
        key_one, key_two = jax.random.split(source_key)
        shuffled = jax.random.permutation(key_one, (DEVICES - 1) * CAP)[:RAW_DEV - CAP]
        others = (shuffled // CAP).astype(jnp.int32)
        others = others + (others >= busiest).astype(jnp.int32)
        chosen = jnp.concatenate([jnp.full((CAP,), busiest, jnp.int32), others])
        return jax.random.permutation(key_two, chosen)
    return jax.vmap(one_source)(source_keys).reshape(DEVICES * RAW_DEV).astype(jnp.int32)


def touch_ends(entries, rng, least, high):
    place = [jax.random.randint(jax.random.fold_in(rng, axis), (), 0, length) for axis, length in enumerate(entries.shape)]
    main_axis = entries.shape.index(max(entries.shape))
    beside = place[:main_axis] + [(place[main_axis] + 1) % entries.shape[main_axis]] + place[main_axis + 1:]
    return entries.at[tuple(place)].set(least).at[tuple(beside)].set(high)


def block_scale(stream_key, dims, shards, smallest, high):
    loudness, own = 1.0, jax.random.fold_in(stream_key, 6)
    for dim, shards_of in shards:
        heights = jnp.exp(jax.random.uniform(jax.random.fold_in(own, dim), (shards_of,), jnp.float32, smallest / len(shards), high / len(shards)))
        loudness = loudness * jnp.repeat(heights, dims[dim] // shards_of).reshape([-1 if axis == dim else 1 for axis in range(len(dims))])
    return loudness


def normal_values(own_key, shape, scale, bound, cuts=(), dtype=jnp.bfloat16):
    drawn = jax.random.normal(own_key, shape, jnp.float32) * scale
    if len(cuts) > 0:
        drawn = block_scale(own_key, shape, cuts, -0.22, 0.18) * drawn
    return jnp.clip(drawn, min=-bound, max=bound).astype(dtype)


def setup_inputs(seed: int = 0) -> dict:
    streams_of = jax.random.split(jax.random.key(seed), 12)
    raw_rows = normal_values(streams_of[0], (DEVICES * RAW_DEV, RAW_COLS), 1.0, 6.0, ((0, 128),))
    raw_wide = touch_ends(jax.random.randint(streams_of[1], (DEVICES * RAW_DEV,), 0, 2), jax.random.fold_in(streams_of[1], 1), 0, 1).astype(jnp.int32)
    raw_dest = draw_raw_dest(jax.random.fold_in(streams_of[11], 71), 0)
    raw_slot = touch_ends(jax.random.randint(streams_of[3], (DEVICES * RAW_DEV,), 0, UPD + IPD), jax.random.fold_in(streams_of[3], 1), 0, (UPD + IPD) - 1).astype(jnp.int32)
    proj_narrow = normal_values(streams_of[4], (NARROW, D), NARROW ** -0.5, 1.0)
    proj_wide = normal_values(streams_of[5], (RAW_COLS, D), RAW_COLS ** -0.5, 0.75)
    adj_values = jnp.clip(jax.random.uniform(streams_of[6], (NU, NI), jnp.float32, -1.0, 1.0) * block_scale(streams_of[6], (NU, NI), ((0, 16), (1, 8)), -0.4, 0.0), -1.0, 1.0).astype(jnp.bfloat16)
    tile_mask = touch_ends((jax.random.randint(streams_of[7], (NU // TILE, NI // TILE), 0, 2) < 1).astype(jnp.int32), jax.random.fold_in(streams_of[7], 1), 0, 1)
    tile_scale = jnp.clip(jnp.exp(math.log(0.041432038) - 2.3025851 * jax.random.uniform(streams_of[8], (NU // TILE, NI // TILE), jnp.float32) ** block_scale(streams_of[8], (NU // TILE, NI // TILE), ((0, 16), (1, 8)), -0.2, 0.2)), 0.0041432036, 0.041432038)
    weight_sum = normal_values(streams_of[9], (LAYERS, D, D), D ** -0.5, 0.5)
    weight_product = normal_values(streams_of[10], (LAYERS, D, D), D ** -0.5, 0.5)
    return dict(raw_rows=raw_rows, raw_wide=raw_wide, raw_dest=raw_dest, raw_slot=raw_slot, proj_narrow=proj_narrow, proj_wide=proj_wide, adj_values=adj_values, tile_mask=tile_mask, tile_scale=tile_scale, weight_sum=weight_sum, weight_product=weight_product)


def dequantize(values_bf, mask_tiles, scale_tiles):
    row_count = values_bf.shape[0]
    columns = values_bf.shape[1]
    values = values_bf.astype(jnp.float32)
    factor = mask_tiles.astype(jnp.float32) * scale_tiles
    tiled = values.reshape(row_count // TILE, TILE, columns // TILE, TILE) * factor[:, None, :, None]
    return tiled.reshape(row_count, columns).astype(jnp.bfloat16)


def update(side_sum, own_rows, weight_sum, weight_product):
    own_float = own_rows.astype(jnp.float32)
    summed = (side_sum + own_float).astype(jnp.bfloat16)
    product = (side_sum * own_float).astype(jnp.bfloat16)
    linear = jnp.dot(summed, weight_sum, preferred_element_type=jnp.float32)
    linear = linear + jnp.dot(product, weight_product, preferred_element_type=jnp.float32)
    return jnp.where(linear > 0, linear, 0.2 * linear).astype(jnp.bfloat16)


def reference(raw_rows, raw_wide, raw_dest, raw_slot, proj_narrow, proj_wide, adj_values, tile_mask, tile_scale, weight_sum, weight_product):
    wide_part = jnp.dot(raw_rows, proj_wide, preferred_element_type=jnp.float32)
    narrow_part = jnp.dot(raw_rows[:, :NARROW], proj_narrow, preferred_element_type=jnp.float32)
    projected = jnp.where((raw_wide == 1)[:, None], wide_part, narrow_part)
    is_user = raw_slot < UPD
    user_index = raw_dest * UPD + raw_slot
    grid_row = raw_dest // N_COL
    grid_col = raw_dest % N_COL
    item_index = grid_col * (IPD * N_ROW) + grid_row * IPD + (raw_slot - UPD)
    target = jnp.where(is_user, user_index, NU + item_index).astype(jnp.int32)
    totals = jax.ops.segment_sum(projected, target, num_segments=NU + NI)
    user_rows = totals[:NU].astype(jnp.bfloat16)
    item_rows = totals[NU:].astype(jnp.bfloat16)
    block_rows = math.gcd(NU, 2048)
    block_count = NU // block_rows
    value_blocks = adj_values.reshape(block_count, block_rows, NI)
    mask_blocks = tile_mask.reshape(block_count, block_rows // TILE, NI // TILE)
    scale_blocks = tile_scale.reshape(block_count, block_rows // TILE, NI // TILE)
    for layer_index in range(LAYERS):
        current_items = item_rows

        def visit_block(item_total, inputs):
            value_block, mask_block, scale_block, user_block = inputs
            adjacency = dequantize(value_block, mask_block, scale_block)
            user_part = jnp.dot(adjacency, current_items, preferred_element_type=jnp.float32)
            item_total = item_total + lax.dot_general(adjacency, user_block, (((0,), (0,)), ((), ())), preferred_element_type=jnp.float32)
            return item_total, user_part

        item_side, user_side = lax.scan(visit_block, jnp.zeros((NI, D), jnp.float32), (value_blocks, mask_blocks, scale_blocks, user_rows.reshape(block_count, block_rows, D)))
        new_users = update(user_side.reshape(NU, D), user_rows, weight_sum[layer_index], weight_product[layer_index])
        new_items = update(item_side, item_rows, weight_sum[layer_index], weight_product[layer_index])
        user_rows = new_users
        item_rows = new_items
    return user_rows, item_rows.reshape(N_COL, IPD * N_ROW, D)
```

```python
import jax
import jax.numpy as jnp
from jax import lax
from jax.experimental import pallas as pl
from jax.experimental.pallas import tpu as pltpu
from jax.sharding import PartitionSpec as P

D = 128
RAW_COLS = 64
NARROW = 32
TILE = 128
LAYERS = 2
UPD = 256
IPD = 256
CAP = 24
ROWS = 16
COLS = 8
DEVICES = ROWS * COLS
RAW_DEV = 1024
USERS = UPD * COLS
ITEMS = IPD * ROWS
NODES = UPD + IPD
GROUP = 16
CHUNK = 768
SIDE = 4
HALF_D = D // 2
SCALED_FIRST = 10
USER_FIRST = 2

F32 = jnp.float32
BF16 = jnp.bfloat16
I32 = jnp.int32
MESH = pl.DeviceIdType.MESH


def dot(a, b):
    return jnp.dot(a, b, preferred_element_type=F32)


def dot_nt(a, b):
    return lax.dot_general(a, b, (((1,), (1,)), ((), ())), preferred_element_type=F32)


def wait_bytes(ref, sem):
    pltpu.make_async_copy(ref, ref, sem).wait()


def update(side, own, weight_sum, weight_product):
    own = own.astype(F32)
    linear = dot((side + own).astype(BF16), weight_sum)
    linear = linear + dot((side * own).astype(BF16), weight_product)
    return jnp.where(linear > 0, linear, 0.2 * linear).astype(BF16)


def kernel(
    raw_hbm,
    wide_hbm,
    dest_hbm,
    slot_hbm,
    narrow_hbm,
    proj_hbm,
    adj_hbm,
    mask_hbm,
    scale_hbm,
    weight_sum_hbm,
    weight_product_hbm,
    user_ref,
    item_ref,
    raw_ref,
    wide_ref,
    dest_ref,
    slot_ref,
    mask_ref,
    scale_ref,
    weight_sum_ref,
    weight_product_ref,
    adj,
    packed,
    place,
    send,
    by_row,
    by_col,
    recv,
    combined,
    totals,
    users,
    items,
    users_t,
    items_all,
    item_send,
    own_a,
    own_b,
    first_a,
    first_b,
    second_send,
    second_a,
    second_b,
    user_send,
    user_recv,
    user_own,
    in_sems,
    adj_sem,
    local_sem,
    row_sems,
    ut_sems,
    ia_sems,
    ir_sems,
    ur_sems,
):
    row = lax.axis_index("row")
    col = lax.axis_index("col")
    x = row // SIDE
    y = lax.rem(row, SIDE)
    row_odd = lax.rem(row, 2)
    col_odd = lax.rem(col, 2)
    odd = lax.rem(row + col, 2)

    inputs = [
        pltpu.make_async_copy(src, dst, in_sems.at[i])
        for i, (src, dst) in enumerate(
            (
                (dest_hbm, dest_ref),
                (slot_hbm, slot_ref),
                (wide_hbm, wide_ref),
                (raw_hbm, raw_ref),
                (mask_hbm, mask_ref),
                (scale_hbm, scale_ref),
                (proj_hbm, combined.at[0:RAW_COLS, :]),
                (narrow_hbm, combined.at[RAW_COLS : RAW_COLS + NARROW, :]),
                (weight_sum_hbm, weight_sum_ref),
                (weight_product_hbm, weight_product_ref),
            )
        )
    ]
    for copy in inputs[:4]:
        copy.start()

    barrier = pltpu.get_barrier_semaphore()

    def greet_row(k, carry):
        there = {"row": lax.rem(row + k, ROWS), "col": col}
        pl.semaphore_signal(barrier, inc=1, device_id=there, device_id_type=MESH)
        return carry

    def greet_col(k, carry):
        there = {"row": row, "col": lax.rem(col + k, COLS)}
        pl.semaphore_signal(barrier, inc=1, device_id=there, device_id_type=MESH)
        return carry

    lax.fori_loop(1, ROWS, greet_row, 0)
    lax.fori_loop(1, COLS, greet_col, 0)

    for copy in inputs[4:]:
        copy.start()

    def adj_copy(i):
        rows = pl.ds(pl.multiple_of(i * TILE, TILE), TILE)
        return pltpu.make_async_copy(adj_hbm.at[rows, :], adj.at[rows, :], adj_sem.at[i])

    def fetch(i, carry):
        adj_copy(i).start()
        return carry

    lax.fori_loop(0, USERS // TILE, fetch, 0)

    def push(src, dst, sems, there):
        pltpu.make_async_remote_copy(
            src_ref=src,
            dst_ref=dst,
            send_sem=sems.at[0],
            recv_sem=sems.at[1],
            device_id=there,
            device_id_type=MESH,
        ).start()

    for copy in inputs[:4]:
        copy.wait()
    dest = dest_ref[...]
    target = lax.broadcasted_iota(I32, (DEVICES, RAW_DEV), 0)
    hit = jnp.where(target == dest, 1.0, 0.0).astype(F32)
    earlier = jnp.where(
        lax.broadcasted_iota(I32, (256, 256), 0) < lax.broadcasted_iota(I32, (256, 256), 1), 1.0, 0.0
    ).astype(BF16)
    before = jnp.zeros((DEVICES, 1), F32)
    device = lax.broadcasted_iota(I32, (DEVICES, 256), 0)
    to_row, to_col = device // COLS, device % COLS
    space = jnp.where(
        (to_row + to_col) % 2 == 0,
        to_row * (COLS // 2) + to_col // 2,
        DEVICES // 2 + to_col * (ROWS // 2) + to_row // 2,
    )
    start = (space * CAP).astype(F32)
    for b in range(RAW_DEV // 256):
        part = hit[:, b * 256 : (b + 1) * 256]
        rank = dot(part.astype(BF16), earlier) + before
        place[0:1, b * 256 : (b + 1) * 256] = jnp.sum(
            part * (rank + start), axis=0, keepdims=True
        ).astype(I32)
        before = before + jnp.sum(part, axis=1, keepdims=True)

    slot = slot_ref[...]
    raw = raw_ref[...].astype(F32)
    wide_f = wide_ref[...].astype(F32)
    packed[0:RAW_COLS, :] = (raw * wide_f).astype(BF16)
    packed[RAW_COLS : RAW_COLS + NARROW, :] = (raw[0:NARROW] * (1.0 - wide_f)).astype(BF16)
    which = lax.broadcasted_iota(I32, (32, RAW_DEV), 0)
    codes = jnp.where(which == 0, slot // 2, jnp.where(which == 1, slot % 2, 0))
    packed[96:128, :] = codes.astype(F32).astype(BF16)

    def build(g):
        first = g * GROUP * CAP
        index = lax.broadcasted_iota(I32, (GROUP * CAP, RAW_DEV), 0) + first
        pick = jnp.where(index == place[0:1, :], 1.0, 0.0).astype(BF16)
        rows = dot_nt(pick, packed[...]).reshape(GROUP, CAP, D).astype(BF16)
        send[pl.ds(pl.multiple_of(g * GROUP, GROUP), GROUP)] = rows

    pl.semaphore_wait(barrier, ROWS + COLS - 2)

    half_row, half_col = COLS // 2, ROWS // 2

    def start_rows(i, carry):
        g = lax.rem(x + i, SIDE)
        build(g)

        def one(k, inner):
            other = g * SIDE + lax.rem(y + k, SIDE)
            src = send.at[pl.ds(pl.multiple_of(other * half_row, half_row), half_row)]

            @pl.when(other != row)
            def _():
                push(src, by_row.at[row], row_sems.at[0], {"row": other, "col": col})

            return inner

        return lax.fori_loop(0, SIDE, one, carry)

    lax.fori_loop(0, SIDE, start_rows, 0)

    def start_cols(i, carry):
        g = lax.rem(col // 2 + i, SIDE)
        build(g + SIDE)

        def one(k, inner):
            other = g * 2 + k
            first = DEVICES // 2 + other * half_col
            src = send.at[pl.ds(pl.multiple_of(first, half_col), half_col)]

            @pl.when(other != col)
            def _():
                push(src, by_col.at[col], row_sems.at[1], {"row": row, "col": other})

            return inner

        return lax.fori_loop(0, 2, one, carry)

    lax.fori_loop(0, SIDE, start_cols, 0)
    my_rows = send.at[pl.ds(pl.multiple_of(row * half_row, half_row), half_row)]
    my_cols = send.at[pl.ds(pl.multiple_of(DEVICES // 2 + col * half_col, half_col), half_col)]
    keep_rows = pltpu.make_async_copy(my_rows, by_row.at[row], local_sem.at[0])
    keep_cols = pltpu.make_async_copy(my_cols, by_col.at[col], local_sem.at[1])
    keep_rows.start()
    keep_cols.start()

    inputs[4].wait()
    inputs[5].wait()

    def scale_tiles(i, carry):
        adj_copy(i).wait()
        rows = pl.ds(pl.multiple_of(i * TILE, TILE), TILE)
        for j in range(ITEMS // TILE):
            factor = mask_ref[i, j].astype(F32) * scale_ref[i, j]
            columns = slice(j * TILE, (j + 1) * TILE)
            adj[rows, columns] = (adj[rows, columns].astype(F32) * factor).astype(BF16)
        return carry

    scaled_first = SCALED_FIRST
    lax.fori_loop(0, scaled_first, scale_tiles, 0)

    keep_rows.wait()
    keep_cols.wait()
    rest_rows = by_row.at[pl.ds(0, ROWS - 1)]
    rest_cols = by_col.at[pl.ds(0, COLS - 1)]
    wait_bytes(rest_rows, row_sems.at[0, 1])

    def along_col(j, carry):
        other = 2 * j + row_odd
        src = by_row.at[:, j]
        dst = recv.at[pl.ds(pl.multiple_of(col * ROWS, ROWS), ROWS)]

        @pl.when(other != col)
        def _():
            push(src, dst, row_sems.at[2], {"row": row, "col": other})

        @pl.when(other == col)
        def _():
            pltpu.make_async_copy(src, dst, local_sem.at[2]).start()

        return carry

    lax.fori_loop(0, half_row, along_col, 0)
    wait_bytes(rest_cols, row_sems.at[1, 1])

    def along_row(j, carry):
        other = 2 * j + 1 - col_odd
        src = by_col.at[:, j]
        dst = recv.at[pl.ds(pl.multiple_of(row * COLS, COLS), COLS)]

        @pl.when(other != row)
        def _():
            push(src, dst, row_sems.at[2], {"row": other, "col": col})

        @pl.when(other == row)
        def _():
            pltpu.make_async_copy(src, dst, local_sem.at[2]).start()

        return carry

    lax.fori_loop(0, half_col, along_row, 0)

    lax.fori_loop(scaled_first, USERS // TILE, scale_tiles, 0)
    combined[96:128, :] = jnp.zeros((32, D), BF16)
    totals[...] = jnp.zeros((NODES, D), F32)
    for copy in inputs[6:]:
        copy.wait()

    @pl.when(odd == 0)
    def _():
        wait_bytes(recv.at[pl.ds(0, ROWS)], local_sem.at[2])
        wait_bytes(recv.at[pl.ds(0, DEVICES - ROWS)], row_sems.at[2, 1])

    @pl.when(odd == 1)
    def _():
        wait_bytes(recv.at[pl.ds(0, COLS)], local_sem.at[2])
        wait_bytes(recv.at[pl.ds(0, DEVICES - COLS)], row_sems.at[2, 1])

    lane = lax.broadcasted_iota(I32, (8, D), 1)
    decode = jnp.where(lane == 96, 2.0, jnp.where(lane == 97, 1.0, 0.0)).astype(BF16)

    def add_chunk(i, carry):
        count = CHUNK // CAP
        rows = recv[pl.ds(pl.multiple_of(i * count, count), count)].reshape(CHUNK, D)
        slots = dot_nt(decode, rows)[0:1, :].astype(I32)
        pick = jnp.where(
            lax.broadcasted_iota(I32, (NODES, CHUNK), 0) == slots, 1.0, 0.0
        ).astype(BF16)
        totals[...] += dot(pick, rows)
        return carry

    lax.fori_loop(0, DEVICES * CAP // CHUNK, add_chunk, 0)
    total = totals[...]
    high = total.astype(BF16)
    left = total - high.astype(F32)
    middle = left.astype(BF16)
    low = (left - middle.astype(F32)).astype(BF16)
    projection = combined[...]
    initial = dot(high, projection) + (dot(middle, projection) + dot(low, projection))
    users[...] = initial[0:UPD].astype(BF16)
    items[...] = initial[UPD:NODES].astype(BF16)

    my_user_lanes = pl.ds(pl.multiple_of(col * UPD, UPD), UPD)

    def send_users(layer):
        users_t[layer, :, my_user_lanes] = jnp.transpose(users[...].astype(F32)).astype(BF16)
        block = users_t.at[layer, :, my_user_lanes]

        def one(k, carry):
            there = {"row": row, "col": lax.rem(col + k, COLS)}
            push(block, block, ut_sems.at[layer], there)
            return carry

        lax.fori_loop(1, COLS, one, 0)

    def ring_x(k):
        return lax.rem(x + k, SIDE) * SIDE + y

    def ring_y(k):
        return x * SIDE + lax.rem(y + k, SIDE)

    def half(layer, block, which):
        first = block * IPD + which * (IPD // 2)
        return items_all.at[layer, pl.ds(pl.multiple_of(first, IPD // 2), IPD // 2), :]

    def send_items(layer):
        items_all[layer, pl.ds(pl.multiple_of(row * IPD, IPD), IPD), :] = items[...]
        top, low_half = half(layer, row, 0), half(layer, row, 1)
        for step, (along, across) in enumerate(((ring_x, ring_y), (ring_y, ring_x))):
            for k in range(1, SIDE):
                push(top, top, ia_sems.at[layer, step], {"row": along(k), "col": col})
                push(low_half, low_half, ia_sems.at[layer, step], {"row": across(k), "col": col})

    def forward_items(layer):
        wait_bytes(items_all.at[layer, pl.ds(0, 3 * IPD), :], ia_sems.at[layer, 0, 1])
        for j in range(1, SIDE):
            top, low_half = half(layer, ring_x(j), 0), half(layer, ring_y(j), 1)
            for k in range(1, SIDE):
                push(top, top, ia_sems.at[layer, 1], {"row": ring_y(k), "col": col})
                push(low_half, low_half, ia_sems.at[layer, 1], {"row": ring_x(k), "col": col})

    def item_block(layer):
        def body(i, carry):
            to_x = lax.rem(x + 1 + i // 2, SIDE)
            first = to_x * SIDE + 2 * lax.rem(i, 2)
            lanes = pl.ds(pl.multiple_of(first * IPD, 2 * IPD), 2 * IPD)
            part = dot(users_t[layer], adj[:, lanes])
            for q in range(2):
                to = first + q
                to_y = lax.rem(to, SIDE)
                block = part[:, q * IPD : (q + 1) * IPD]
                item_send[to] = block.astype(BF16)

                @pl.when(to_y != y)
                def _():
                    ahead = lax.rem(to_y - y + SIDE, SIDE)
                    there = {"row": x * SIDE + to_y, "col": col}
                    push(
                        item_send.at[to, 0:HALF_D],
                        first_a.at[layer, ahead - 1, to_x],
                        ir_sems.at[layer, 0],
                        there,
                    )

                @pl.when(to_y == y)
                def _():
                    own_a[to_x] = block[0:HALF_D]

                @pl.when(to_x != x)
                def _():
                    ahead = lax.rem(to_x - x + SIDE, SIDE)
                    there = {"row": to_x * SIDE + y, "col": col}
                    push(
                        item_send.at[to, HALF_D:D],
                        first_b.at[layer, ahead - 1, to_y],
                        ir_sems.at[layer, 1],
                        there,
                    )

                @pl.when(to_x == x)
                def _():
                    own_b[to_y] = block[HALF_D:D]

            return carry

        lax.fori_loop(0, ROWS // 2, body, 0)

    def forward_sums(layer):
        wait_bytes(first_a.at[layer], ir_sems.at[layer, 0, 1])
        wait_bytes(first_b.at[layer], ir_sems.at[layer, 1, 1])
        for k in range(1, SIDE):
            to_x, to_y = lax.rem(x + k, SIDE), lax.rem(y + k, SIDE)
            for h, (own, came, to, there, land) in enumerate(
                (
                    (own_a, first_a, to_x, ring_x(k), second_a),
                    (own_b, first_b, to_y, ring_y(k), second_b),
                )
            ):
                total = own[to]
                for source in range(SIDE - 1):
                    total = total + came[layer, source, to].astype(F32)
                second_send[k - 1, h] = total.astype(BF16)
                push(
                    second_send.at[k - 1, h],
                    land.at[layer, k - 1],
                    ir_sems.at[layer, 2],
                    {"row": there, "col": col},
                )

    def item_side(layer):
        halves = []
        sums = ((own_a, first_a, x), (own_b, first_b, y))
        for own, came, here in sums:
            total = own[here]
            for source in range(SIDE - 1):
                total = total + came[layer, source, here].astype(F32)
            halves.append(total)
        wait_bytes(second_send, ir_sems.at[layer, 2, 1])
        for h, land in enumerate((second_a, second_b)):
            for source in range(SIDE - 1):
                halves[h] = halves[h] + land[layer, source].astype(F32)
        return jnp.transpose(jnp.concatenate(halves, axis=0))

    def user_block(layer):
        def body(i, carry):
            first = 2 * lax.rem(col // 2 + 1 + i, SIDE)
            rows = pl.ds(pl.multiple_of(first * UPD, 2 * UPD), 2 * UPD)
            part = dot(adj[rows, :], items_all[layer])
            for q in range(2):
                to = first + q
                block = part[q * UPD : (q + 1) * UPD]

                @pl.when(to != col)
                def _():
                    ahead = lax.rem(to - col + COLS, COLS)
                    user_send[ahead - 1] = block.astype(BF16)
                    push(
                        user_send.at[ahead - 1],
                        user_recv.at[layer, ahead - 1],
                        ur_sems.at[layer],
                        {"row": row, "col": to},
                    )

                @pl.when(to == col)
                def _():
                    user_own[...] = block

            return carry

        return body

    send_users(0)
    send_items(0)
    for layer in range(LAYERS):
        last = layer + 1 == LAYERS
        forward_items(layer)
        users_in = users_t.at[layer, :, pl.ds(0, (COLS - 1) * UPD)]
        wait_bytes(users_in, ut_sems.at[layer, 1])
        item_block(layer)
        second_in = items_all.at[layer, pl.ds(0, 12 * IPD), :]
        wait_bytes(second_in, ia_sems.at[layer, 1, 1])
        lax.fori_loop(0, USER_FIRST, user_block(layer), 0)
        forward_sums(layer)
        lax.fori_loop(USER_FIRST, SIDE, user_block(layer), 0)

        new_items = update(
            item_side(layer), items[...], weight_sum_ref[layer], weight_product_ref[layer]
        )
        if last:
            item_ref[...] = new_items
        else:
            items[...] = new_items
            send_items(layer + 1)

        wait_bytes(user_recv.at[layer], ur_sems.at[layer, 1])
        side = user_own[...]
        for k in range(COLS - 1):
            side = side + user_recv[layer, k].astype(F32)
        new_users = update(side, users[...], weight_sum_ref[layer], weight_product_ref[layer])
        if last:
            user_ref[...] = new_users
        else:
            users[...] = new_users
            send_users(layer + 1)

        wait_bytes(users_in, ut_sems.at[layer, 0])
        wait_bytes(items_all.at[layer, pl.ds(0, 3 * IPD), :], ia_sems.at[layer, 0, 0])
        wait_bytes(second_in, ia_sems.at[layer, 1, 0])
        wait_bytes(first_a.at[layer], ir_sems.at[layer, 0, 0])
        wait_bytes(first_b.at[layer], ir_sems.at[layer, 1, 0])
        wait_bytes(second_send, ir_sems.at[layer, 2, 0])
        wait_bytes(user_send, ur_sems.at[layer, 0])

    wait_bytes(rest_rows, row_sems.at[0, 0])
    wait_bytes(rest_cols, row_sems.at[1, 0])

    @pl.when(odd == 0)
    def _():
        wait_bytes(recv.at[pl.ds(0, DEVICES - ROWS)], row_sems.at[2, 0])

    @pl.when(odd == 1)
    def _():
        wait_bytes(recv.at[pl.ds(0, DEVICES - COLS)], row_sems.at[2, 0])


def per_device(
    raw_rows,
    raw_wide,
    raw_dest,
    raw_slot,
    proj_narrow,
    proj_wide,
    adj_values,
    tile_mask,
    tile_scale,
    weight_sum,
    weight_product,
):
    vmem = pl.BlockSpec(memory_space=pltpu.VMEM)
    hbm = pl.BlockSpec(memory_space=pltpu.HBM)
    dma = pltpu.SemaphoreType.DMA
    user_rows, item_rows = pl.pallas_call(
        kernel,
        out_shape=(
            jax.ShapeDtypeStruct((UPD, D), BF16),
            jax.ShapeDtypeStruct((IPD, D), BF16),
        ),
        in_specs=[hbm] * 11,
        out_specs=(vmem, vmem),
        scratch_shapes=[
            pltpu.VMEM((RAW_COLS, RAW_DEV), BF16),
            pltpu.VMEM((1, RAW_DEV), I32),
            pltpu.VMEM((1, RAW_DEV), I32),
            pltpu.VMEM((1, RAW_DEV), I32),
            pltpu.SMEM((USERS // TILE, ITEMS // TILE), I32),
            pltpu.SMEM((USERS // TILE, ITEMS // TILE), F32),
            pltpu.VMEM((LAYERS, D, D), BF16),
            pltpu.VMEM((LAYERS, D, D), BF16),
            pltpu.VMEM((USERS, ITEMS), BF16),
            pltpu.VMEM((D, RAW_DEV), BF16),
            pltpu.VMEM((8, RAW_DEV), I32),
            pltpu.VMEM((DEVICES, CAP, D), BF16),
            pltpu.VMEM((ROWS, COLS // 2, CAP, D), BF16),
            pltpu.VMEM((COLS, ROWS // 2, CAP, D), BF16),
            pltpu.VMEM((DEVICES, CAP, D), BF16),
            pltpu.VMEM((D, D), BF16),
            pltpu.VMEM((NODES, D), F32),
            pltpu.VMEM((UPD, D), BF16),
            pltpu.VMEM((IPD, D), BF16),
            pltpu.VMEM((LAYERS, D, USERS), BF16),
            pltpu.VMEM((LAYERS, ITEMS, D), BF16),
            pltpu.VMEM((ROWS, D, IPD), BF16),
            pltpu.VMEM((SIDE, HALF_D, IPD), F32),
            pltpu.VMEM((SIDE, HALF_D, IPD), F32),
            pltpu.VMEM((LAYERS, SIDE - 1, SIDE, HALF_D, IPD), BF16),
            pltpu.VMEM((LAYERS, SIDE - 1, SIDE, HALF_D, IPD), BF16),
            pltpu.VMEM((SIDE - 1, 2, HALF_D, IPD), BF16),
            pltpu.VMEM((LAYERS, SIDE - 1, HALF_D, IPD), BF16),
            pltpu.VMEM((LAYERS, SIDE - 1, HALF_D, IPD), BF16),
            pltpu.VMEM((COLS - 1, UPD, D), BF16),
            pltpu.VMEM((LAYERS, COLS - 1, UPD, D), BF16),
            pltpu.VMEM((UPD, D), F32),
            dma((10,)),
            dma((USERS // TILE,)),
            dma((3,)),
            dma((3, 2)),
            dma((LAYERS, 2)),
            dma((LAYERS, 2, 2)),
            dma((LAYERS, 3, 2)),
            dma((LAYERS, 2)),
        ],
        compiler_params=pltpu.CompilerParams(
            collective_id=0, has_side_effects=True, vmem_limit_bytes=56 << 20
        ),
    )(
        raw_rows.T,
        raw_wide.reshape(1, RAW_DEV),
        raw_dest.reshape(1, RAW_DEV),
        raw_slot.reshape(1, RAW_DEV),
        proj_narrow,
        proj_wide,
        adj_values,
        tile_mask,
        tile_scale,
        weight_sum,
        weight_product,
    )
    return (user_rows, item_rows[None])


def solution(mesh):
    placed = (
        P(("row", "col"), None),
        P(("row", "col")),
        P(("row", "col")),
        P(("row", "col")),
        P(),
        P(),
        P("row", "col"),
        P("row", "col"),
        P("row", "col"),
        P(),
        P(),
    )
    return jax.shard_map(
        per_device,
        mesh=mesh,
        in_specs=placed,
        out_specs=(P(("row", "col"), None), P("col", "row", None)),
        check_vma=False,
    )
```

```python
import jax
import jax.numpy as jnp
from jax import lax
from jax.experimental import pallas as pl
from jax.experimental.pallas import tpu as pltpu
from jax.sharding import PartitionSpec as P

D = 128
RAW_COLS = 64
NARROW = 32
TILE = 128
LAYERS = 2
UPD = 256
IPD = 256
CAP = 24
ROWS = 16
COLS = 8
DEVICES = ROWS * COLS
RAW_DEV = 1024
USERS = UPD * COLS
ITEMS = IPD * ROWS
NODES = UPD + IPD
GROUP = 16
CHUNK = 768
SIDE = 4
HALF_D = D // 2
SCALED_FIRST = 10

F32 = jnp.float32
BF16 = jnp.bfloat16
I32 = jnp.int32
MESH = pl.DeviceIdType.MESH


def dot(a, b):
    return jnp.dot(a, b, preferred_element_type=F32)


def dot_nt(a, b):
    return lax.dot_general(a, b, (((1,), (1,)), ((), ())), preferred_element_type=F32)


def wait_bytes(ref, sem):
    pltpu.make_async_copy(ref, ref, sem).wait()


def update(side, own, weight_sum, weight_product):
    own = own.astype(F32)
    linear = dot((side + own).astype(BF16), weight_sum)
    linear = linear + dot((side * own).astype(BF16), weight_product)
    return jnp.where(linear > 0, linear, 0.2 * linear).astype(BF16)


def kernel(
    raw_hbm,
    wide_hbm,
    dest_hbm,
    slot_hbm,
    narrow_hbm,
    proj_hbm,
    adj_hbm,
    mask_hbm,
    scale_hbm,
    weight_sum_hbm,
    weight_product_hbm,
    user_ref,
    item_ref,
    raw_ref,
    wide_ref,
    dest_ref,
    slot_ref,
    mask_ref,
    scale_ref,
    weight_sum_ref,
    weight_product_ref,
    adj,
    packed,
    place,
    send,
    by_row,
    by_col,
    recv,
    combined,
    totals,
    users,
    items,
    users_t,
    items_all,
    item_send,
    own_a,
    own_b,
    first_a,
    first_b,
    second_send,
    second_a,
    second_b,
    user_send,
    user_recv,
    user_own,
    in_sems,
    adj_sem,
    local_sem,
    row_send,
    row_recv,
    chunk_sem,
    ut_send,
    ut_recv,
    ia_send,
    ia_recv,
    ir_send,
    ir_recv,
    ur_sems,
):
    row = lax.axis_index("row")
    col = lax.axis_index("col")
    x = row // SIDE
    y = lax.rem(row, SIDE)
    z = col // 2
    row_odd = lax.rem(row, 2)
    col_odd = lax.rem(col, 2)
    odd = lax.rem(row + col, 2)

    inputs = [
        pltpu.make_async_copy(src, dst, in_sems.at[i])
        for i, (src, dst) in enumerate(
            (
                (dest_hbm, dest_ref),
                (slot_hbm, slot_ref),
                (wide_hbm, wide_ref),
                (raw_hbm, raw_ref),
                (mask_hbm, mask_ref),
                (scale_hbm, scale_ref),
                (proj_hbm, combined.at[0:RAW_COLS, :]),
                (narrow_hbm, combined.at[RAW_COLS : RAW_COLS + NARROW, :]),
                (weight_sum_hbm, weight_sum_ref),
                (weight_product_hbm, weight_product_ref),
            )
        )
    ]
    for copy in inputs[:4]:
        copy.start()

    barrier = pltpu.get_barrier_semaphore()

    def greet_row(k, carry):
        there = {"row": lax.rem(row + k, ROWS), "col": col}
        pl.semaphore_signal(barrier, inc=1, device_id=there, device_id_type=MESH)
        return carry

    def greet_col(k, carry):
        there = {"row": row, "col": lax.rem(col + k, COLS)}
        pl.semaphore_signal(barrier, inc=1, device_id=there, device_id_type=MESH)
        return carry

    lax.fori_loop(1, ROWS, greet_row, 0)
    lax.fori_loop(1, COLS, greet_col, 0)

    for copy in inputs[4:]:
        copy.start()

    def adj_copy(i):
        rows = pl.ds(pl.multiple_of(i * TILE, TILE), TILE)
        return pltpu.make_async_copy(adj_hbm.at[rows, :], adj.at[rows, :], adj_sem.at[i])

    def fetch(i, carry):
        adj_copy(i).start()
        return carry

    lax.fori_loop(0, USERS // TILE, fetch, 0)

    def push(src, dst, send_sem, recv_sem, there):
        pltpu.make_async_remote_copy(
            src_ref=src,
            dst_ref=dst,
            send_sem=send_sem,
            recv_sem=recv_sem,
            device_id=there,
            device_id_type=MESH,
        ).start()

    for copy in inputs[:4]:
        copy.wait()
    dest = dest_ref[...]
    target = lax.broadcasted_iota(I32, (DEVICES, RAW_DEV), 0)
    hit = jnp.where(target == dest, 1.0, 0.0).astype(F32)
    earlier = jnp.where(
        lax.broadcasted_iota(I32, (256, 256), 0) < lax.broadcasted_iota(I32, (256, 256), 1), 1.0, 0.0
    ).astype(BF16)
    before = jnp.zeros((DEVICES, 1), F32)
    device = lax.broadcasted_iota(I32, (DEVICES, 256), 0)
    to_row, to_col = device // COLS, device % COLS
    space = jnp.where(
        (to_row + to_col) % 2 == 0,
        to_row * (COLS // 2) + to_col // 2,
        DEVICES // 2 + to_col * (ROWS // 2) + to_row // 2,
    )
    start = (space * CAP).astype(F32)
    for b in range(RAW_DEV // 256):
        part = hit[:, b * 256 : (b + 1) * 256]
        rank = dot(part.astype(BF16), earlier) + before
        place[0:1, b * 256 : (b + 1) * 256] = jnp.sum(
            part * (rank + start), axis=0, keepdims=True
        ).astype(I32)
        before = before + jnp.sum(part, axis=1, keepdims=True)

    slot = slot_ref[...]
    raw = raw_ref[...].astype(F32)
    wide_f = wide_ref[...].astype(F32)
    packed[0:RAW_COLS, :] = (raw * wide_f).astype(BF16)
    packed[RAW_COLS : RAW_COLS + NARROW, :] = (raw[0:NARROW] * (1.0 - wide_f)).astype(BF16)
    which = lax.broadcasted_iota(I32, (32, RAW_DEV), 0)
    codes = jnp.where(which == 0, slot // 2, jnp.where(which == 1, slot % 2, 0))
    packed[96:128, :] = codes.astype(F32).astype(BF16)

    def build(g):
        first = g * GROUP * CAP
        index = lax.broadcasted_iota(I32, (GROUP * CAP, RAW_DEV), 0) + first
        pick = jnp.where(index == place[0:1, :], 1.0, 0.0).astype(BF16)
        rows = dot_nt(pick, packed[...]).reshape(GROUP, CAP, D).astype(BF16)
        send[pl.ds(pl.multiple_of(g * GROUP, GROUP), GROUP)] = rows

    def build_rows(g, carry):
        build(g)
        return carry

    lax.fori_loop(0, SIDE, build_rows, 0)
    pl.semaphore_wait(barrier, ROWS + COLS - 2)

    half_row, half_col = COLS // 2, ROWS // 2

    def start_rows(k, carry):
        other = lax.rem(row + k, ROWS)
        src = send.at[pl.ds(pl.multiple_of(other * half_row, half_row), half_row)]
        there = {"row": other, "col": col}
        push(src, by_row.at[row], row_send.at[0], row_recv.at[0], there)
        return carry

    lax.fori_loop(1, ROWS, start_rows, 0)

    def start_cols(i, carry):
        g = lax.rem(col // 2 + i, SIDE)
        build(g + SIDE)

        def one(k, inner):
            other = g * 2 + k
            first = DEVICES // 2 + other * half_col
            src = send.at[pl.ds(pl.multiple_of(first, half_col), half_col)]

            @pl.when(other != col)
            def _():
                there = {"row": row, "col": other}
                push(src, by_col.at[col], row_send.at[1], row_recv.at[1], there)

            return inner

        return lax.fori_loop(0, 2, one, carry)

    lax.fori_loop(0, SIDE, start_cols, 0)
    my_rows = send.at[pl.ds(pl.multiple_of(row * half_row, half_row), half_row)]
    my_cols = send.at[pl.ds(pl.multiple_of(DEVICES // 2 + col * half_col, half_col), half_col)]
    keep_rows = pltpu.make_async_copy(my_rows, by_row.at[row], local_sem.at[0])
    keep_cols = pltpu.make_async_copy(my_cols, by_col.at[col], local_sem.at[1])
    keep_rows.start()
    keep_cols.start()

    inputs[4].wait()
    inputs[5].wait()

    def scale_tiles(i, carry):
        adj_copy(i).wait()
        rows = pl.ds(pl.multiple_of(i * TILE, TILE), TILE)
        for j in range(ITEMS // TILE):
            factor = mask_ref[i, j].astype(F32) * scale_ref[i, j]
            columns = slice(j * TILE, (j + 1) * TILE)
            adj[rows, columns] = (adj[rows, columns].astype(F32) * factor).astype(BF16)
        return carry

    scaled_first = SCALED_FIRST
    lax.fori_loop(0, scaled_first, scale_tiles, 0)

    keep_rows.wait()
    keep_cols.wait()
    rest_rows = by_row.at[pl.ds(0, ROWS - 1)]
    rest_cols = by_col.at[pl.ds(0, COLS - 1)]
    wait_bytes(rest_rows, row_recv.at[0])

    def along_col(j, carry):
        other = 2 * j + row_odd
        src = by_row.at[:, j]
        dst = recv.at[pl.ds(pl.multiple_of(col * ROWS, ROWS), ROWS)]

        @pl.when(other != col)
        def _():
            push(src, dst, row_send.at[2], chunk_sem.at[z], {"row": row, "col": other})

        @pl.when(other == col)
        def _():
            pltpu.make_async_copy(src, dst, local_sem.at[2]).start()

        return carry

    lax.fori_loop(0, half_row, along_col, 0)
    wait_bytes(rest_cols, row_recv.at[1])

    def along_row(j, carry):
        other = 2 * j + 1 - col_odd
        src = by_col.at[:, j]
        dst = recv.at[pl.ds(pl.multiple_of(row * COLS, COLS), COLS)]

        @pl.when(other != row)
        def _():
            push(src, dst, row_send.at[2], chunk_sem.at[x], {"row": other, "col": col})

        @pl.when(other == row)
        def _():
            pltpu.make_async_copy(src, dst, local_sem.at[2]).start()

        return carry

    lax.fori_loop(0, half_col, along_row, 0)

    lax.fori_loop(scaled_first, USERS // TILE, scale_tiles, 0)
    combined[96:128, :] = jnp.zeros((32, D), BF16)
    for copy in inputs[6:]:
        copy.wait()

    lane = lax.broadcasted_iota(I32, (8, D), 1)
    decode = jnp.where(lane == 96, 2.0, jnp.where(lane == 97, 1.0, 0.0)).astype(BF16)

    def add_chunk(i):
        count = CHUNK // CAP
        rows = recv[pl.ds(pl.multiple_of(i * count, count), count)].reshape(CHUNK, D)
        slots = dot_nt(decode, rows)[0:1, :].astype(I32)
        pick = jnp.where(
            lax.broadcasted_iota(I32, (NODES, CHUNK), 0) == slots, 1.0, 0.0
        ).astype(BF16)
        return dot(pick, rows)

    nearest = odd * x + (1 - odd) * z

    @pl.when(odd == 0)
    def _():
        wait_bytes(recv.at[pl.ds(0, ROWS)], local_sem.at[2])
        wait_bytes(recv.at[pl.ds(0, ROWS)], chunk_sem.at[nearest])

    @pl.when(odd == 1)
    def _():
        wait_bytes(recv.at[pl.ds(0, COLS)], local_sem.at[2])
        wait_bytes(recv.at[pl.ds(0, 3 * COLS)], chunk_sem.at[nearest])

    totals[...] = add_chunk(nearest)
    for step in (1, 3, 2):
        chunk = lax.rem(nearest + step, SIDE)
        wait_bytes(recv.at[pl.ds(0, DEVICES // SIDE)], chunk_sem.at[chunk])
        totals[...] += add_chunk(chunk)
    total = totals[...]
    high = total.astype(BF16)
    left = total - high.astype(F32)
    middle = left.astype(BF16)
    low = (left - middle.astype(F32)).astype(BF16)
    projection = combined[...]
    initial = dot(high, projection) + (dot(middle, projection) + dot(low, projection))
    users[...] = initial[0:UPD].astype(BF16)
    items[...] = initial[UPD:NODES].astype(BF16)

    my_user_lanes = pl.ds(pl.multiple_of(col * UPD, UPD), UPD)

    def user_lanes(layer, owner):
        lanes = pl.ds(pl.multiple_of(owner * UPD, UPD), UPD)
        return users_t.at[layer, :, lanes]

    partner = {"row": row, "col": col + 1 - 2 * col_odd}

    def send_users(layer):
        users_t[layer, :, my_user_lanes] = jnp.transpose(users[...].astype(F32)).astype(BF16)
        block = user_lanes(layer, col)
        for k in (1, 3, 2):
            there = {"row": row, "col": lax.rem(col + 2 * k, COLS)}
            push(block, block, ut_send.at[layer, 0], ut_recv.at[layer, k], there)
        push(block, block, ut_send.at[layer, 1], ut_recv.at[layer, 0], partner)

    def forward_users(layer, k):
        block = user_lanes(layer, lax.rem(col + COLS - 2 * k, COLS))
        wait_bytes(block, ut_recv.at[layer, k])
        push(block, block, ut_send.at[layer, 1], ut_recv.at[layer, 0], partner)

    def ring_x(k):
        return lax.rem(x + k, SIDE) * SIDE + y

    def ring_y(k):
        return x * SIDE + lax.rem(y + k, SIDE)

    def half(layer, block, which):
        first = block * IPD + which * (IPD // 2)
        return items_all.at[layer, pl.ds(pl.multiple_of(first, IPD // 2), IPD // 2), :]

    def send_items(layer):
        items_all[layer, pl.ds(pl.multiple_of(row * IPD, IPD), IPD), :] = items[...]
        top, bottom = half(layer, row, 0), half(layer, row, 1)
        for k in (1, 3, 2):
            along, across = {"row": ring_x(k), "col": col}, {"row": ring_y(k), "col": col}
            push(top, top, ia_send.at[layer, 0], ia_recv.at[layer, 0, k], along)
            push(bottom, bottom, ia_send.at[layer, 0], ia_recv.at[layer, 1, k], across)
        for k in (1, 3, 2):
            along, across = {"row": ring_x(k), "col": col}, {"row": ring_y(k), "col": col}
            push(top, top, ia_send.at[layer, 1], ia_recv.at[layer, 0, 0], across)
            push(bottom, bottom, ia_send.at[layer, 1], ia_recv.at[layer, 1, 0], along)

    def forward_items(layer, j):
        top, bottom = half(layer, ring_x(SIDE - j), 0), half(layer, ring_y(SIDE - j), 1)
        wait_bytes(top, ia_recv.at[layer, 0, j])
        for k in (1, 3, 2):
            across = {"row": ring_y(k), "col": col}
            push(top, top, ia_send.at[layer, 1], ia_recv.at[layer, 0, 0], across)
        wait_bytes(bottom, ia_recv.at[layer, 1, j])
        for k in (1, 3, 2):
            along = {"row": ring_x(k), "col": col}
            push(bottom, bottom, ia_send.at[layer, 1], ia_recv.at[layer, 1, 0], along)

    def item_block(layer):
        def body(i, carry):
            to_x = lax.rem(x + 1 + i // 2, SIDE)
            first = to_x * SIDE + 2 * lax.rem(i, 2)
            lanes = pl.ds(pl.multiple_of(first * IPD, 2 * IPD), 2 * IPD)
            part = dot(users_t[layer], adj[:, lanes])
            for q in range(2):
                to = first + q
                to_y = lax.rem(to, SIDE)
                block = part[:, q * IPD : (q + 1) * IPD]
                item_send[to] = block.astype(BF16)

                @pl.when(to_y != y)
                def _():
                    ahead = lax.rem(to_y - y + SIDE, SIDE)
                    there = {"row": x * SIDE + to_y, "col": col}
                    push(
                        item_send.at[to, 0:HALF_D],
                        first_a.at[layer, ahead - 1, to_x],
                        ir_send.at[layer, 0],
                        ir_recv.at[layer, 0, to_x],
                        there,
                    )

                @pl.when(to_y == y)
                def _():
                    own_a[to_x] = block[0:HALF_D]

                @pl.when(to_x != x)
                def _():
                    ahead = lax.rem(to_x - x + SIDE, SIDE)
                    there = {"row": to_x * SIDE + y, "col": col}
                    push(
                        item_send.at[to, HALF_D:D],
                        first_b.at[layer, ahead - 1, to_y],
                        ir_send.at[layer, 0],
                        ir_recv.at[layer, 1, to_y],
                        there,
                    )

                @pl.when(to_x == x)
                def _():
                    own_b[to_y] = block[HALF_D:D]

            return carry

        lax.fori_loop(0, ROWS // 2, body, 0)

    def first_sum(layer, h, to):
        own, came = ((own_a, first_a), (own_b, first_b))[h]
        wait_bytes(second_send.at[:, 0], ir_recv.at[layer, h, to])
        total = own[to]
        for source in range(SIDE - 1):
            total = total + came[layer, source, to].astype(F32)
        return total

    def forward_sum(layer, h, k):
        to = lax.rem((x, y)[h] + k, SIDE)
        second_send[k - 1, h] = first_sum(layer, h, to).astype(BF16)
        push(
            second_send.at[k - 1, h],
            (second_a, second_b)[h].at[layer, k - 1],
            ir_send.at[layer, 1],
            ir_recv.at[layer, 2, 0],
            {"row": (ring_x, ring_y)[h](k), "col": col},
        )

    def item_side(layer):
        halves = [first_sum(layer, 0, x), first_sum(layer, 1, y)]
        wait_bytes(second_send, ir_recv.at[layer, 2, 0])
        for h, land in enumerate((second_a, second_b)):
            for source in range(SIDE - 1):
                halves[h] = halves[h] + land[layer, source].astype(F32)
        return jnp.transpose(jnp.concatenate(halves, axis=0))

    def user_block(layer):
        def body(i, carry):
            first = 2 * lax.rem(col // 2 + 1 + i, SIDE)
            rows = pl.ds(pl.multiple_of(first * UPD, 2 * UPD), 2 * UPD)
            part = dot(adj[rows, :], items_all[layer])
            for q in range(2):
                to = first + q
                block = part[q * UPD : (q + 1) * UPD]

                @pl.when(to != col)
                def _():
                    ahead = lax.rem(to - col + COLS, COLS)
                    user_send[ahead - 1] = block.astype(BF16)
                    push(
                        user_send.at[ahead - 1],
                        user_recv.at[layer, ahead - 1],
                        ur_sems.at[layer, 0],
                        ur_sems.at[layer, 1],
                        {"row": row, "col": to},
                    )

                @pl.when(to == col)
                def _():
                    user_own[...] = block

            return carry

        return body

    send_users(0)
    send_items(0)
    for layer in range(LAYERS):
        last = layer + 1 == LAYERS
        for k in (1, 3, 2):
            forward_items(layer, k)
        for k in (1, 3, 2):
            forward_users(layer, k)
        wait_bytes(users_t.at[layer, :, pl.ds(0, 4 * UPD)], ut_recv.at[layer, 0])
        item_block(layer)
        gathered = items_all.at[layer, pl.ds(0, 6 * IPD), :]
        wait_bytes(gathered, ia_recv.at[layer, 0, 0])
        wait_bytes(gathered, ia_recv.at[layer, 1, 0])
        blocks = user_block(layer)
        lax.fori_loop(0, 3, blocks, 0)
        forward_sum(layer, 0, 1)
        forward_sum(layer, 0, 2)
        forward_sum(layer, 0, 3)
        forward_sum(layer, 1, 1)
        forward_sum(layer, 1, 2)
        forward_sum(layer, 1, 3)
        lax.fori_loop(3, 4, blocks, 0)

        new_items = update(
            item_side(layer), items[...], weight_sum_ref[layer], weight_product_ref[layer]
        )
        if last:
            item_ref[...] = new_items
        else:
            items[...] = new_items
            send_items(layer + 1)

        wait_bytes(user_recv.at[layer], ur_sems.at[layer, 1])
        side = user_own[...]
        for k in range(COLS - 1):
            side = side + user_recv[layer, k].astype(F32)
        new_users = update(side, users[...], weight_sum_ref[layer], weight_product_ref[layer])
        if last:
            user_ref[...] = new_users
        else:
            users[...] = new_users
            send_users(layer + 1)

        wait_bytes(users_t.at[layer, :, pl.ds(0, 3 * UPD)], ut_send.at[layer, 0])
        wait_bytes(users_t.at[layer, :, pl.ds(0, 4 * UPD)], ut_send.at[layer, 1])
        wait_bytes(items_all.at[layer, pl.ds(0, 3 * IPD), :], ia_send.at[layer, 0])
        wait_bytes(items_all.at[layer, pl.ds(0, 12 * IPD), :], ia_send.at[layer, 1])
        wait_bytes(first_a.at[layer], ir_send.at[layer, 0])
        wait_bytes(first_b.at[layer], ir_send.at[layer, 0])
        wait_bytes(second_send, ir_send.at[layer, 1])
        wait_bytes(user_send, ur_sems.at[layer, 0])

    wait_bytes(rest_rows, row_send.at[0])
    wait_bytes(rest_cols, row_send.at[1])

    @pl.when(odd == 0)
    def _():
        wait_bytes(recv.at[pl.ds(0, DEVICES - ROWS)], row_send.at[2])

    @pl.when(odd == 1)
    def _():
        wait_bytes(recv.at[pl.ds(0, DEVICES - COLS)], row_send.at[2])


def per_device(
    raw_rows,
    raw_wide,
    raw_dest,
    raw_slot,
    proj_narrow,
    proj_wide,
    adj_values,
    tile_mask,
    tile_scale,
    weight_sum,
    weight_product,
):
    vmem = pl.BlockSpec(memory_space=pltpu.VMEM)
    hbm = pl.BlockSpec(memory_space=pltpu.HBM)
    dma = pltpu.SemaphoreType.DMA
    user_rows, item_rows = pl.pallas_call(
        kernel,
        out_shape=(pltpu.VMEM((UPD, D), BF16), pltpu.VMEM((IPD, D), BF16)),
        in_specs=[hbm] * 11,
        out_specs=(vmem, vmem),
        scratch_shapes=[
            pltpu.VMEM((RAW_COLS, RAW_DEV), BF16),
            pltpu.VMEM((1, RAW_DEV), I32),
            pltpu.VMEM((1, RAW_DEV), I32),
            pltpu.VMEM((1, RAW_DEV), I32),
            pltpu.SMEM((USERS // TILE, ITEMS // TILE), I32),
            pltpu.SMEM((USERS // TILE, ITEMS // TILE), F32),
            pltpu.VMEM((LAYERS, D, D), BF16),
            pltpu.VMEM((LAYERS, D, D), BF16),
            pltpu.VMEM((USERS, ITEMS), BF16),
            pltpu.VMEM((D, RAW_DEV), BF16),
            pltpu.VMEM((8, RAW_DEV), I32),
            pltpu.VMEM((DEVICES, CAP, D), BF16),
            pltpu.VMEM((ROWS, COLS // 2, CAP, D), BF16),
            pltpu.VMEM((COLS, ROWS // 2, CAP, D), BF16),
            pltpu.VMEM((DEVICES, CAP, D), BF16),
            pltpu.VMEM((D, D), BF16),
            pltpu.VMEM((NODES, D), F32),
            pltpu.VMEM((UPD, D), BF16),
            pltpu.VMEM((IPD, D), BF16),
            pltpu.VMEM((LAYERS, D, USERS), BF16),
            pltpu.VMEM((LAYERS, ITEMS, D), BF16),
            pltpu.VMEM((ROWS, D, IPD), BF16),
            pltpu.VMEM((SIDE, HALF_D, IPD), F32),
            pltpu.VMEM((SIDE, HALF_D, IPD), F32),
            pltpu.VMEM((LAYERS, SIDE - 1, SIDE, HALF_D, IPD), BF16),
            pltpu.VMEM((LAYERS, SIDE - 1, SIDE, HALF_D, IPD), BF16),
            pltpu.VMEM((SIDE - 1, 2, HALF_D, IPD), BF16),
            pltpu.VMEM((LAYERS, SIDE - 1, HALF_D, IPD), BF16),
            pltpu.VMEM((LAYERS, SIDE - 1, HALF_D, IPD), BF16),
            pltpu.VMEM((COLS - 1, UPD, D), BF16),
            pltpu.VMEM((LAYERS, COLS - 1, UPD, D), BF16),
            pltpu.VMEM((UPD, D), F32),
            dma((10,)),
            dma((USERS // TILE,)),
            dma((3,)),
            dma((3,)),
            dma((2,)),
            dma((SIDE,)),
            dma((LAYERS, 2)),
            dma((LAYERS, SIDE)),
            dma((LAYERS, 2)),
            dma((LAYERS, 2, SIDE)),
            dma((LAYERS, 2)),
            dma((LAYERS, 3, SIDE)),
            dma((LAYERS, 2)),
        ],
        compiler_params=pltpu.CompilerParams(
            collective_id=0, has_side_effects=True, vmem_limit_bytes=56 << 20
        ),
    )(
        raw_rows.T,
        raw_wide.reshape(1, RAW_DEV),
        raw_dest.reshape(1, RAW_DEV),
        raw_slot.reshape(1, RAW_DEV),
        proj_narrow,
        proj_wide,
        adj_values,
        tile_mask,
        tile_scale,
        weight_sum,
        weight_product,
    )
    return (user_rows, item_rows[None])


def solution(mesh):
    placed = (
        P(("row", "col"), None),
        P(("row", "col")),
        P(("row", "col")),
        P(("row", "col")),
        P(),
        P(),
        P("row", "col"),
        P("row", "col"),
        P("row", "col"),
        P(),
        P(),
    )
    return jax.shard_map(
        per_device,
        mesh=mesh,
        in_specs=placed,
        out_specs=(P(("row", "col"), None), P("col", "row", None)),
        check_vma=False,
    )
```

```python
import jax
import jax.numpy as jnp
from jax import lax
from jax.experimental import pallas as pl
from jax.experimental.pallas import tpu as pltpu
from jax.sharding import PartitionSpec as P

D = 128
RAW_COLS = 64
NARROW = 32
TILE = 128
LAYERS = 2
UPD = 256
IPD = 256
CAP = 24
ROWS = 16
COLS = 8
DEVICES = ROWS * COLS
RAW_DEV = 1024
USERS = UPD * COLS
ITEMS = IPD * ROWS
NODES = UPD + IPD
GROUP = 16
CHUNK = 768
SIDE = 4
HALF_D = D // 2
SCALED_STEP = 2

F32 = jnp.float32
BF16 = jnp.bfloat16
I32 = jnp.int32
MESH = pl.DeviceIdType.MESH


def dot(a, b):
    return jnp.dot(a, b, preferred_element_type=F32)


def dot_nt(a, b):
    return lax.dot_general(a, b, (((1,), (1,)), ((), ())), preferred_element_type=F32)


def wait_bytes(ref, sem):
    pltpu.make_async_copy(ref, ref, sem).wait()


def update(side, own, weight_sum, weight_product):
    own = own.astype(F32)
    linear = dot((side + own).astype(BF16), weight_sum)
    linear = linear + dot((side * own).astype(BF16), weight_product)
    return jnp.where(linear > 0, linear, 0.2 * linear).astype(BF16)


def kernel(
    raw_hbm,
    wide_hbm,
    dest_hbm,
    slot_hbm,
    narrow_hbm,
    proj_hbm,
    adj_hbm,
    mask_hbm,
    scale_hbm,
    weight_sum_hbm,
    weight_product_hbm,
    user_ref,
    item_ref,
    raw_ref,
    wide_ref,
    dest_ref,
    slot_ref,
    mask_ref,
    scale_ref,
    weight_sum_ref,
    weight_product_ref,
    adj,
    packed,
    place,
    send,
    by_row,
    by_col,
    recv,
    combined,
    totals,
    users,
    items,
    users_t,
    items_all,
    item_send,
    own_a,
    own_b,
    first_a,
    first_b,
    second_send,
    second_a,
    second_b,
    user_send,
    user_recv,
    user_own,
    in_sems,
    adj_sem,
    local_sem,
    row_send,
    row_recv,
    chunk_sem,
    ut_send,
    ut_recv,
    ia_send,
    ia_recv,
    ir_send,
    ir_recv,
    ur_sems,
):
    row = lax.axis_index("row")
    col = lax.axis_index("col")
    x = row // SIDE
    y = lax.rem(row, SIDE)
    z = col // 2
    row_odd = lax.rem(row, 2)
    col_odd = lax.rem(col, 2)
    odd = lax.rem(row + col, 2)

    inputs = [
        pltpu.make_async_copy(src, dst, in_sems.at[i])
        for i, (src, dst) in enumerate(
            (
                (dest_hbm, dest_ref),
                (slot_hbm, slot_ref),
                (wide_hbm, wide_ref),
                (raw_hbm, raw_ref),
                (mask_hbm, mask_ref),
                (scale_hbm, scale_ref),
                (proj_hbm, combined.at[0:RAW_COLS, :]),
                (narrow_hbm, combined.at[RAW_COLS : RAW_COLS + NARROW, :]),
                (weight_sum_hbm, weight_sum_ref),
                (weight_product_hbm, weight_product_ref),
            )
        )
    ]
    for copy in inputs[:4]:
        copy.start()

    barrier = pltpu.get_barrier_semaphore()

    def greet_row(k, carry):
        there = {"row": lax.rem(row + k, ROWS), "col": col}
        pl.semaphore_signal(barrier, inc=1, device_id=there, device_id_type=MESH)
        return carry

    def greet_col(k, carry):
        there = {"row": row, "col": lax.rem(col + k, COLS)}
        pl.semaphore_signal(barrier, inc=1, device_id=there, device_id_type=MESH)
        return carry

    lax.fori_loop(1, ROWS, greet_row, 0)
    lax.fori_loop(1, COLS, greet_col, 0)

    for copy in inputs[4:]:
        copy.start()

    def adj_copy(i):
        rows = pl.ds(pl.multiple_of(i * TILE, TILE), TILE)
        return pltpu.make_async_copy(adj_hbm.at[rows, :], adj.at[rows, :], adj_sem.at[i])

    def fetch(i, carry):
        adj_copy(i).start()
        return carry

    lax.fori_loop(0, USERS // TILE, fetch, 0)

    def push(src, dst, send_sem, recv_sem, there):
        pltpu.make_async_remote_copy(
            src_ref=src,
            dst_ref=dst,
            send_sem=send_sem,
            recv_sem=recv_sem,
            device_id=there,
            device_id_type=MESH,
        ).start()

    for copy in inputs[:4]:
        copy.wait()
    dest = dest_ref[...]
    target = lax.broadcasted_iota(I32, (DEVICES, RAW_DEV), 0)
    hit = jnp.where(target == dest, 1.0, 0.0).astype(F32)
    earlier = jnp.where(
        lax.broadcasted_iota(I32, (256, 256), 0) < lax.broadcasted_iota(I32, (256, 256), 1), 1.0, 0.0
    ).astype(BF16)
    before = jnp.zeros((DEVICES, 1), F32)
    device = lax.broadcasted_iota(I32, (DEVICES, 256), 0)
    to_row, to_col = device // COLS, device % COLS
    space = jnp.where(
        (to_row + to_col) % 2 == 0,
        to_row * (COLS // 2) + to_col // 2,
        DEVICES // 2 + to_col * (ROWS // 2) + to_row // 2,
    )
    start = (space * CAP).astype(F32)
    for b in range(RAW_DEV // 256):
        part = hit[:, b * 256 : (b + 1) * 256]
        rank = dot(part.astype(BF16), earlier) + before
        place[0:1, b * 256 : (b + 1) * 256] = jnp.sum(
            part * (rank + start), axis=0, keepdims=True
        ).astype(I32)
        before = before + jnp.sum(part, axis=1, keepdims=True)

    slot = slot_ref[...]
    raw = raw_ref[...].astype(F32)
    wide_f = wide_ref[...].astype(F32)
    packed[0:RAW_COLS, :] = (raw * wide_f).astype(BF16)
    packed[RAW_COLS : RAW_COLS + NARROW, :] = (raw[0:NARROW] * (1.0 - wide_f)).astype(BF16)
    which = lax.broadcasted_iota(I32, (32, RAW_DEV), 0)
    codes = jnp.where(which == 0, slot // 2, jnp.where(which == 1, slot % 2, 0))
    packed[96:128, :] = codes.astype(F32).astype(BF16)

    def build(g):
        first = g * GROUP * CAP
        index = lax.broadcasted_iota(I32, (GROUP * CAP, RAW_DEV), 0) + first
        pick = jnp.where(index == place[0:1, :], 1.0, 0.0).astype(BF16)
        rows = dot_nt(pick, packed[...]).reshape(GROUP, CAP, D).astype(BF16)
        send[pl.ds(pl.multiple_of(g * GROUP, GROUP), GROUP)] = rows

    def build_rows(g, carry):
        build(g)
        return carry

    lax.fori_loop(0, SIDE, build_rows, 0)
    pl.semaphore_wait(barrier, ROWS + COLS - 2)

    half_row, half_col = COLS // 2, ROWS // 2

    def start_rows(k, carry):
        other = lax.rem(row + k, ROWS)
        src = send.at[pl.ds(pl.multiple_of(other * half_row, half_row), half_row)]
        there = {"row": other, "col": col}
        push(src, by_row.at[row], row_send.at[0], row_recv.at[0, x], there)
        return carry

    lax.fori_loop(1, ROWS, start_rows, 0)

    def start_cols(i, carry):
        g = lax.rem(col // 2 + i, SIDE)
        build(g + SIDE)

        def one(k, inner):
            other = g * 2 + k
            first = DEVICES // 2 + other * half_col
            src = send.at[pl.ds(pl.multiple_of(first, half_col), half_col)]

            @pl.when(other != col)
            def _():
                there = {"row": row, "col": other}
                push(src, by_col.at[col], row_send.at[1], row_recv.at[1, z], there)

            return inner

        return lax.fori_loop(0, 2, one, carry)

    lax.fori_loop(0, SIDE, start_cols, 0)
    my_rows = send.at[pl.ds(pl.multiple_of(row * half_row, half_row), half_row)]
    my_cols = send.at[pl.ds(pl.multiple_of(DEVICES // 2 + col * half_col, half_col), half_col)]
    keep_rows = pltpu.make_async_copy(my_rows, by_row.at[row], local_sem.at[0])
    keep_cols = pltpu.make_async_copy(my_cols, by_col.at[col], local_sem.at[1])
    keep_rows.start()
    keep_cols.start()

    inputs[4].wait()
    inputs[5].wait()

    def scale_tiles(i, carry):
        adj_copy(i).wait()
        rows = pl.ds(pl.multiple_of(i * TILE, TILE), TILE)
        for j in range(ITEMS // TILE):
            factor = mask_ref[i, j].astype(F32) * scale_ref[i, j]
            columns = slice(j * TILE, (j + 1) * TILE)
            adj[rows, columns] = (adj[rows, columns].astype(F32) * factor).astype(BF16)
        return carry

    rest_rows = by_row.at[pl.ds(0, ROWS - 1)]
    rest_cols = by_col.at[pl.ds(0, COLS - 1)]

    def along_col(g):
        sources = pl.ds(pl.multiple_of(g * SIDE, SIDE), SIDE)
        landing = recv.at[pl.ds(pl.multiple_of(col * ROWS + g * SIDE, SIDE), SIDE)]

        def one(j, carry):
            other = 2 * j + row_odd
            src = by_row.at[sources, j]

            @pl.when(other != col)
            def _():
                push(src, landing, row_send.at[2], chunk_sem.at[z], {"row": row, "col": other})

            @pl.when(other == col)
            def _():
                pltpu.make_async_copy(src, landing, local_sem.at[2]).start()

            return carry

        lax.fori_loop(0, half_row, one, 0)

    def along_row(g):
        sources = pl.ds(pl.multiple_of(g * 2, 2), 2)
        landing = recv.at[pl.ds(pl.multiple_of(row * COLS + g * 2, 2), 2)]

        def one(j, carry):
            other = 2 * j + 1 - col_odd
            src = by_col.at[sources, j]

            @pl.when(other != row)
            def _():
                push(src, landing, row_send.at[2], chunk_sem.at[x], {"row": other, "col": col})

            @pl.when(other == row)
            def _():
                pltpu.make_async_copy(src, landing, local_sem.at[2]).start()

            return carry

        lax.fori_loop(0, half_col, one, 0)

    scaled = 0
    for step in (0, 1, 3, 2):
        lax.fori_loop(scaled, scaled + SCALED_STEP, scale_tiles, 0)
        scaled += SCALED_STEP
        from_x, from_z = lax.rem(x + step, SIDE), lax.rem(z + step, SIDE)
        if step == 0:
            keep_rows.wait()
            keep_cols.wait()
        near = 1 if step == 0 else 0
        wait_bytes(by_col.at[pl.ds(0, 2 - near)], row_recv.at[1, from_z])
        along_row(from_z)
        wait_bytes(by_row.at[pl.ds(0, SIDE - near)], row_recv.at[0, from_x])
        along_col(from_x)

    lax.fori_loop(scaled, USERS // TILE, scale_tiles, 0)
    combined[96:128, :] = jnp.zeros((32, D), BF16)
    for copy in inputs[6:]:
        copy.wait()

    lane = lax.broadcasted_iota(I32, (8, D), 1)
    decode = jnp.where(lane == 96, 2.0, jnp.where(lane == 97, 1.0, 0.0)).astype(BF16)

    def add_chunk(i):
        count = CHUNK // CAP
        rows = recv[pl.ds(pl.multiple_of(i * count, count), count)].reshape(CHUNK, D)
        slots = dot_nt(decode, rows)[0:1, :].astype(I32)
        pick = jnp.where(
            lax.broadcasted_iota(I32, (NODES, CHUNK), 0) == slots, 1.0, 0.0
        ).astype(BF16)
        return dot(pick, rows)

    nearest = odd * x + (1 - odd) * z

    @pl.when(odd == 0)
    def _():
        wait_bytes(recv.at[pl.ds(0, ROWS)], local_sem.at[2])
        wait_bytes(recv.at[pl.ds(0, ROWS)], chunk_sem.at[nearest])

    @pl.when(odd == 1)
    def _():
        wait_bytes(recv.at[pl.ds(0, COLS)], local_sem.at[2])
        wait_bytes(recv.at[pl.ds(0, 3 * COLS)], chunk_sem.at[nearest])

    totals[...] = add_chunk(nearest)
    for step in (1, 3, 2):
        chunk = lax.rem(nearest + step, SIDE)
        wait_bytes(recv.at[pl.ds(0, DEVICES // SIDE)], chunk_sem.at[chunk])
        totals[...] += add_chunk(chunk)
    total = totals[...]
    high = total.astype(BF16)
    left = total - high.astype(F32)
    middle = left.astype(BF16)
    low = (left - middle.astype(F32)).astype(BF16)
    projection = combined[...]
    initial = dot(high, projection) + (dot(middle, projection) + dot(low, projection))
    users[...] = initial[0:UPD].astype(BF16)
    items[...] = initial[UPD:NODES].astype(BF16)

    my_user_lanes = pl.ds(pl.multiple_of(col * UPD, UPD), UPD)

    def user_lanes(layer, owner):
        lanes = pl.ds(pl.multiple_of(owner * UPD, UPD), UPD)
        return users_t.at[layer, :, lanes]

    partner = {"row": row, "col": col + 1 - 2 * col_odd}

    def send_users(layer):
        users_t[layer, :, my_user_lanes] = jnp.transpose(users[...].astype(F32)).astype(BF16)
        block = user_lanes(layer, col)
        for k in (1, 3, 2):
            there = {"row": row, "col": lax.rem(col + 2 * k, COLS)}
            push(block, block, ut_send.at[layer, 0], ut_recv.at[layer, k], there)
        push(block, block, ut_send.at[layer, 1], ut_recv.at[layer, 0], partner)

    def forward_users(layer, k):
        block = user_lanes(layer, lax.rem(col + COLS - 2 * k, COLS))
        wait_bytes(block, ut_recv.at[layer, k])
        push(block, block, ut_send.at[layer, 1], ut_recv.at[layer, 0], partner)

    def ring_x(k):
        return lax.rem(x + k, SIDE) * SIDE + y

    def ring_y(k):
        return x * SIDE + lax.rem(y + k, SIDE)

    def half(layer, block, which):
        first = block * IPD + which * (IPD // 2)
        return items_all.at[layer, pl.ds(pl.multiple_of(first, IPD // 2), IPD // 2), :]

    def send_items(layer):
        items_all[layer, pl.ds(pl.multiple_of(row * IPD, IPD), IPD), :] = items[...]
        top, bottom = half(layer, row, 0), half(layer, row, 1)
        for k in (1, 3, 2):
            along, across = {"row": ring_x(k), "col": col}, {"row": ring_y(k), "col": col}
            push(top, top, ia_send.at[layer, 0], ia_recv.at[layer, 0, k], along)
            push(bottom, bottom, ia_send.at[layer, 0], ia_recv.at[layer, 1, k], across)
        for k in (1, 3, 2):
            along, across = {"row": ring_x(k), "col": col}, {"row": ring_y(k), "col": col}
            push(top, top, ia_send.at[layer, 1], ia_recv.at[layer, 0, 0], across)
            push(bottom, bottom, ia_send.at[layer, 1], ia_recv.at[layer, 1, 0], along)

    def forward_items(layer, j):
        top, bottom = half(layer, ring_x(SIDE - j), 0), half(layer, ring_y(SIDE - j), 1)
        wait_bytes(top, ia_recv.at[layer, 0, j])
        for k in (1, 3, 2):
            across = {"row": ring_y(k), "col": col}
            push(top, top, ia_send.at[layer, 1], ia_recv.at[layer, 0, 0], across)
        wait_bytes(bottom, ia_recv.at[layer, 1, j])
        for k in (1, 3, 2):
            along = {"row": ring_x(k), "col": col}
            push(bottom, bottom, ia_send.at[layer, 1], ia_recv.at[layer, 1, 0], along)

    def item_block(layer):
        def body(i, carry):
            to_x = lax.rem(x + 1 + i // 2, SIDE)
            first = to_x * SIDE + 2 * lax.rem(i, 2)
            lanes = pl.ds(pl.multiple_of(first * IPD, 2 * IPD), 2 * IPD)
            part = dot(users_t[layer], adj[:, lanes])
            for q in range(2):
                to = first + q
                to_y = lax.rem(to, SIDE)
                block = part[:, q * IPD : (q + 1) * IPD]
                item_send[to] = block.astype(BF16)

                @pl.when(to_y != y)
                def _():
                    ahead = lax.rem(to_y - y + SIDE, SIDE)
                    there = {"row": x * SIDE + to_y, "col": col}
                    push(
                        item_send.at[to, 0:HALF_D],
                        first_a.at[layer, ahead - 1, to_x],
                        ir_send.at[layer, 0],
                        ir_recv.at[layer, 0, to_x],
                        there,
                    )

                @pl.when(to_y == y)
                def _():
                    own_a[to_x] = block[0:HALF_D]

                @pl.when(to_x != x)
                def _():
                    ahead = lax.rem(to_x - x + SIDE, SIDE)
                    there = {"row": to_x * SIDE + y, "col": col}
                    push(
                        item_send.at[to, HALF_D:D],
                        first_b.at[layer, ahead - 1, to_y],
                        ir_send.at[layer, 0],
                        ir_recv.at[layer, 1, to_y],
                        there,
                    )

                @pl.when(to_x == x)
                def _():
                    own_b[to_y] = block[HALF_D:D]

            return carry

        lax.fori_loop(0, ROWS // 2, body, 0)

    def first_sum(layer, h, to):
        own, came = ((own_a, first_a), (own_b, first_b))[h]
        wait_bytes(second_send.at[:, 0], ir_recv.at[layer, h, to])
        total = own[to]
        for source in range(SIDE - 1):
            total = total + came[layer, source, to].astype(F32)
        return total

    def forward_sum(layer, h, k):
        to = lax.rem((x, y)[h] + k, SIDE)
        second_send[k - 1, h] = first_sum(layer, h, to).astype(BF16)
        push(
            second_send.at[k - 1, h],
            (second_a, second_b)[h].at[layer, k - 1],
            ir_send.at[layer, 1],
            ir_recv.at[layer, 2, 0],
            {"row": (ring_x, ring_y)[h](k), "col": col},
        )

    def item_side(layer):
        halves = [first_sum(layer, 0, x), first_sum(layer, 1, y)]
        wait_bytes(second_send, ir_recv.at[layer, 2, 0])
        for h, land in enumerate((second_a, second_b)):
            for source in range(SIDE - 1):
                halves[h] = halves[h] + land[layer, source].astype(F32)
        return jnp.transpose(jnp.concatenate(halves, axis=0))

    def user_block(layer):
        def body(i, carry):
            first = 2 * lax.rem(col // 2 + 1 + i, SIDE)
            rows = pl.ds(pl.multiple_of(first * UPD, 2 * UPD), 2 * UPD)
            part = dot(adj[rows, :], items_all[layer])
            for q in range(2):
                to = first + q
                block = part[q * UPD : (q + 1) * UPD]

                @pl.when(to != col)
                def _():
                    ahead = lax.rem(to - col + COLS, COLS)
                    user_send[ahead - 1] = block.astype(BF16)
                    push(
                        user_send.at[ahead - 1],
                        user_recv.at[layer, ahead - 1],
                        ur_sems.at[layer, 0],
                        ur_sems.at[layer, 1],
                        {"row": row, "col": to},
                    )

                @pl.when(to == col)
                def _():
                    user_own[...] = block

            return carry

        return body

    send_users(0)
    send_items(0)
    for layer in range(LAYERS):
        last = layer + 1 == LAYERS
        for k in (1, 3, 2):
            forward_items(layer, k)
        for k in (1, 3, 2):
            forward_users(layer, k)
        wait_bytes(users_t.at[layer, :, pl.ds(0, 4 * UPD)], ut_recv.at[layer, 0])
        item_block(layer)
        gathered = items_all.at[layer, pl.ds(0, 6 * IPD), :]
        wait_bytes(gathered, ia_recv.at[layer, 0, 0])
        wait_bytes(gathered, ia_recv.at[layer, 1, 0])
        blocks = user_block(layer)
        lax.fori_loop(0, 3, blocks, 0)
        forward_sum(layer, 0, 1)
        forward_sum(layer, 0, 2)
        forward_sum(layer, 0, 3)
        forward_sum(layer, 1, 1)
        forward_sum(layer, 1, 2)
        forward_sum(layer, 1, 3)
        lax.fori_loop(3, 4, blocks, 0)

        new_items = update(
            item_side(layer), items[...], weight_sum_ref[layer], weight_product_ref[layer]
        )
        if last:
            item_ref[...] = new_items
        else:
            items[...] = new_items
            send_items(layer + 1)

        wait_bytes(user_recv.at[layer], ur_sems.at[layer, 1])
        side = user_own[...]
        for k in range(COLS - 1):
            side = side + user_recv[layer, k].astype(F32)
        new_users = update(side, users[...], weight_sum_ref[layer], weight_product_ref[layer])
        if last:
            user_ref[...] = new_users
        else:
            users[...] = new_users
            send_users(layer + 1)

        wait_bytes(users_t.at[layer, :, pl.ds(0, 3 * UPD)], ut_send.at[layer, 0])
        wait_bytes(users_t.at[layer, :, pl.ds(0, 4 * UPD)], ut_send.at[layer, 1])
        wait_bytes(items_all.at[layer, pl.ds(0, 3 * IPD), :], ia_send.at[layer, 0])
        wait_bytes(items_all.at[layer, pl.ds(0, 12 * IPD), :], ia_send.at[layer, 1])
        wait_bytes(first_a.at[layer], ir_send.at[layer, 0])
        wait_bytes(first_b.at[layer], ir_send.at[layer, 0])
        wait_bytes(second_send, ir_send.at[layer, 1])
        wait_bytes(user_send, ur_sems.at[layer, 0])

    wait_bytes(rest_rows, row_send.at[0])
    wait_bytes(rest_cols, row_send.at[1])

    @pl.when(odd == 0)
    def _():
        wait_bytes(recv.at[pl.ds(0, DEVICES - ROWS)], row_send.at[2])

    @pl.when(odd == 1)
    def _():
        wait_bytes(recv.at[pl.ds(0, DEVICES - COLS)], row_send.at[2])


def per_device(
    raw_rows,
    raw_wide,
    raw_dest,
    raw_slot,
    proj_narrow,
    proj_wide,
    adj_values,
    tile_mask,
    tile_scale,
    weight_sum,
    weight_product,
):
    vmem = pl.BlockSpec(memory_space=pltpu.VMEM)
    hbm = pl.BlockSpec(memory_space=pltpu.HBM)
    dma = pltpu.SemaphoreType.DMA
    user_rows, item_rows = pl.pallas_call(
        kernel,
        out_shape=(pltpu.VMEM((UPD, D), BF16), pltpu.VMEM((IPD, D), BF16)),
        in_specs=[hbm] * 11,
        out_specs=(vmem, vmem),
        scratch_shapes=[
            pltpu.VMEM((RAW_COLS, RAW_DEV), BF16),
            pltpu.VMEM((1, RAW_DEV), I32),
            pltpu.VMEM((1, RAW_DEV), I32),
            pltpu.VMEM((1, RAW_DEV), I32),
            pltpu.SMEM((USERS // TILE, ITEMS // TILE), I32),
            pltpu.SMEM((USERS // TILE, ITEMS // TILE), F32),
            pltpu.VMEM((LAYERS, D, D), BF16),
            pltpu.VMEM((LAYERS, D, D), BF16),
            pltpu.VMEM((USERS, ITEMS), BF16),
            pltpu.VMEM((D, RAW_DEV), BF16),
            pltpu.VMEM((8, RAW_DEV), I32),
            pltpu.VMEM((DEVICES, CAP, D), BF16),
            pltpu.VMEM((ROWS, COLS // 2, CAP, D), BF16),
            pltpu.VMEM((COLS, ROWS // 2, CAP, D), BF16),
            pltpu.VMEM((DEVICES, CAP, D), BF16),
            pltpu.VMEM((D, D), BF16),
            pltpu.VMEM((NODES, D), F32),
            pltpu.VMEM((UPD, D), BF16),
            pltpu.VMEM((IPD, D), BF16),
            pltpu.VMEM((LAYERS, D, USERS), BF16),
            pltpu.VMEM((LAYERS, ITEMS, D), BF16),
            pltpu.VMEM((ROWS, D, IPD), BF16),
            pltpu.VMEM((SIDE, HALF_D, IPD), F32),
            pltpu.VMEM((SIDE, HALF_D, IPD), F32),
            pltpu.VMEM((LAYERS, SIDE - 1, SIDE, HALF_D, IPD), BF16),
            pltpu.VMEM((LAYERS, SIDE - 1, SIDE, HALF_D, IPD), BF16),
            pltpu.VMEM((SIDE - 1, 2, HALF_D, IPD), BF16),
            pltpu.VMEM((LAYERS, SIDE - 1, HALF_D, IPD), BF16),
            pltpu.VMEM((LAYERS, SIDE - 1, HALF_D, IPD), BF16),
            pltpu.VMEM((COLS - 1, UPD, D), BF16),
            pltpu.VMEM((LAYERS, COLS - 1, UPD, D), BF16),
            pltpu.VMEM((UPD, D), F32),
            dma((10,)),
            dma((USERS // TILE,)),
            dma((3,)),
            dma((3,)),
            dma((2, SIDE)),
            dma((SIDE,)),
            dma((LAYERS, 2)),
            dma((LAYERS, SIDE)),
            dma((LAYERS, 2)),
            dma((LAYERS, 2, SIDE)),
            dma((LAYERS, 2)),
            dma((LAYERS, 3, SIDE)),
            dma((LAYERS, 2)),
        ],
        compiler_params=pltpu.CompilerParams(
            collective_id=0, has_side_effects=True, vmem_limit_bytes=56 << 20
        ),
    )(
        raw_rows.T,
        raw_wide.reshape(1, RAW_DEV),
        raw_dest.reshape(1, RAW_DEV),
        raw_slot.reshape(1, RAW_DEV),
        proj_narrow,
        proj_wide,
        adj_values,
        tile_mask,
        tile_scale,
        weight_sum,
        weight_product,
    )
    return (user_rows, item_rows[None])


def solution(mesh):
    placed = (
        P(("row", "col"), None),
        P(("row", "col")),
        P(("row", "col")),
        P(("row", "col")),
        P(),
        P(),
        P("row", "col"),
        P("row", "col"),
        P("row", "col"),
        P(),
        P(),
    )
    return jax.shard_map(
        per_device,
        mesh=mesh,
        in_specs=placed,
        out_specs=(P(("row", "col"), None), P("col", "row", None)),
        check_vma=False,
    )
```
